32 devices in a mesh: dp: 8 (over z, x), seq: 4 (over y, core).
Axes of the slice: x: 2, y: 2, z: 4, core: 2. Of those that a mesh axis runs over, the one named last changes fastest.
Arguments:
- query_rows: bfloat16 [4096, 4096], P(('dp', 'seq')), may hold values from -60 to 60
- key_rows: bfloat16 [4096, 4096], P(('dp', 'seq')), may hold values from -5 to 5
- value_rows: bfloat16 [4096, 4096], P(('dp', 'seq')), may hold values from -12 to 12
- seg_ids: int32 [4096], P(('dp', 'seq')), may hold values from 0 to 15, as said below
- timesteps: int32 [16], replicated, may hold values from 0 to 999
- w_mod: bfloat16 [256, 4096], replicated, may hold values from -0.375 to 0.375
Outputs:
- mixed_rows: bfloat16 [4096, 4096], P(('dp', 'seq'))
The draws below stay inside these ranges and needn't reach their ends.
Inputs may be any that keep to these rules, and one draw needn't show every extreme that they name: A row's bin is seg_ids // 2, a number below the size of dp. The 128 rows of one device hold at most 32 rows of any one bin, and for every index of seq some bin holds exactly 32 rows on each device of that index. Rows of one sample lie on many devices.
All inputs are finite; a program needn't handle non-finite values.
Results may differ from the reference program's by a relative error of at most 0.0058.
Values may be sent and summed in bfloat16 or wider, within the bound.
A program may use at most 128 MiB of HBM per device.

```python
import math
import jax
import jax.numpy as jnp
from jax import lax

HEADS = 32
HEAD_DIM = 128
D = 4096
FREQ = 256
TOK_DEV = 128
SEG_BIN = 2
BIN_SLOTS = 1024
ROWS = 4096
SAMPLES = 16
N_DP = 8
N_SEQ = 4


def seg_layout(key):
    devices = N_DP * N_SEQ
    mean_rows = TOK_DEV // N_DP
    key_base = jax.random.fold_in(key, 11)
    full_bins = jax.random.randint(jax.random.fold_in(key_base, 1), (N_SEQ,), 0, N_DP)

    def one_device(device):
        dev_key = jax.random.fold_in(key_base, 100 + device)
        sub_keys = jax.random.split(dev_key, 4)
        full_bin = full_bins[device % N_SEQ]
        bin_scores = jax.random.randint(sub_keys[0], (N_DP,), 0, 1 << 16) * N_DP + jnp.arange(N_DP)
        bin_scores = jnp.where(jnp.arange(N_DP) == full_bin, -1, bin_scores)
        bin_order = jnp.argsort(bin_scores)
        shifts = jax.random.randint(sub_keys[1], (N_DP // 2,), 0, mean_rows + 1)
        shifts = shifts.at[0].set(mean_rows)
        count_sorted = jnp.stack([mean_rows + shifts, mean_rows - shifts], axis=1).reshape(-1)
        bounds = jnp.cumsum(count_sorted)
        positions = jnp.arange(TOK_DEV)
        bin_slot = jnp.sum((positions[:, None] >= bounds[None, :]).astype(jnp.int32), axis=1)
        row_bins = bin_order[bin_slot]
        groups = jax.random.randint(sub_keys[2], (TOK_DEV,), 0, SEG_BIN)
        groups = groups.at[1].set(groups[0])
        sample_ids = row_bins * SEG_BIN + groups
        shuffle_scores = jax.random.randint(sub_keys[3], (TOK_DEV,), 0, 1 << 16) * TOK_DEV + positions
        shuffle = jnp.argsort(shuffle_scores)
        inverse = jnp.argsort(shuffle)
        return (sample_ids[shuffle], inverse[0], inverse[1])
    return jax.vmap(one_device)(jnp.arange(devices))


def draw_seg_ids(key, part):
    sample_ids, first_row, second_row = seg_layout(key)
    return sample_ids.reshape(-1).astype(jnp.int32)


def draw_key_rows(key, part):
    devices = N_DP * N_SEQ
    row_data = jnp.clip(jax.random.normal(jax.random.fold_in(key, 29), (devices, TOK_DEV, D), jnp.float32), -4.5, 4.5)
    return row_data.reshape(devices * TOK_DEV, D).astype(jnp.bfloat16)


def draw_query_rows(key, part):
    devices = N_DP * N_SEQ
    key_base = jax.random.fold_in(key, 31)
    row_data = jnp.clip(jax.random.normal(key_base, (devices, TOK_DEV, D), jnp.float32), -4.5, 4.5)
    return row_data.reshape(devices * TOK_DEV, D).astype(jnp.bfloat16)


def plant(drawn, key, least, top_value):
    dims = drawn.shape
    index_at = [jax.random.randint(jax.random.fold_in(key, axis), (), 0, dims[axis]) for axis in range(len(dims))]
    drawn = drawn.at[tuple(index_at)].set(least)
    longest = dims.index(max(dims))
    index_at[longest] = (index_at[longest] + 1) % dims[longest]
    return drawn.at[tuple(index_at)].set(top_value)


def shard_levels(own_key, dims, cuts, smallest, top_value):
    def one(dim, blocks):
        steps = jax.random.uniform(jax.random.fold_in(jax.random.fold_in(own_key, 6), dim), (blocks,), jnp.float32, smallest / len(cuts), top_value / len(cuts))
        return jnp.repeat(jnp.exp(steps), dims[dim] // blocks).reshape((-1,) + (1,) * (len(dims) - dim - 1))

    loudness = one(*cuts[0])
    for cut in cuts[1:]:
        loudness = loudness * one(*cut)
    return loudness


def scatter_about(rng, extent, deviation, limit, pieces=(), kind=jnp.bfloat16):
    factor_of = shard_levels(rng, extent, pieces, -0.22, 0.18) if pieces else 1.0
    values = jax.random.normal(rng, extent, jnp.float32) * deviation * factor_of
    return jnp.minimum(jnp.maximum(values, -limit), limit).astype(kind)


def setup_inputs(seed: int = 0) -> dict:
    arg_keys = jax.random.split(jax.random.key(seed), 7)
    query_rows = draw_query_rows(jax.random.fold_in(arg_keys[6], 71), 0)
    key_rows = draw_key_rows(jax.random.fold_in(arg_keys[6], 71), 0)
    value_rows = scatter_about(arg_keys[2], (ROWS, D), 2.0, 12.0, ((0, 32),))
    seg_ids = draw_seg_ids(jax.random.fold_in(arg_keys[6], 71), 0)
    timesteps = plant(jax.random.randint(arg_keys[4], (SAMPLES,), 0, 1000), jax.random.fold_in(arg_keys[4], 1), 0, 999).astype(jnp.int32)
    w_mod = scatter_about(arg_keys[5], (FREQ, D), FREQ ** -0.5, 0.375)
    return dict(query_rows=query_rows, key_rows=key_rows, value_rows=value_rows, seg_ids=seg_ids, timesteps=timesteps, w_mod=w_mod)


def scale_rows_table(timesteps, w_mod):
    half_freq = FREQ // 2
    frequencies = jnp.exp(-math.log(10000.0) * jnp.arange(half_freq, dtype=jnp.float32) / half_freq)
    angles = timesteps.astype(jnp.float32)[:, None] * frequencies[None, :]
    embedding = jnp.concatenate([jnp.cos(angles), jnp.sin(angles)], axis=1)
    activated = jax.nn.silu(embedding).astype(jnp.bfloat16)
    return jnp.dot(activated, w_mod, preferred_element_type=jnp.float32)

def attend_bin(query_part, key_part, value_part, sample_ids):
    score_scale = 1.0 / math.sqrt(HEAD_DIM)
    same_sample = sample_ids[:, None] == sample_ids[None, :]

    def one_head(head_start):
        head_query = lax.dynamic_slice_in_dim(query_part, head_start, HEAD_DIM, 1)
        head_key = lax.dynamic_slice_in_dim(key_part, head_start, HEAD_DIM, 1)
        head_value = lax.dynamic_slice_in_dim(value_part, head_start, HEAD_DIM, 1)
        scores = jnp.dot(head_query, head_key.T, preferred_element_type=jnp.float32) * score_scale
        scores = jnp.where(same_sample, scores, -1e+30)
        row_max = lax.optimization_barrier(jnp.max(scores, axis=1, keepdims=True))
        weights = jnp.exp(scores - row_max)
        soft_probs = (weights / lax.optimization_barrier(jnp.sum(weights, axis=1, keepdims=True))).astype(jnp.bfloat16)
        return jnp.dot(soft_probs, head_value, preferred_element_type=jnp.float32).astype(jnp.bfloat16)
    head_starts = jnp.arange(HEADS, dtype=jnp.int32) * HEAD_DIM
    per_head = lax.map(one_head, head_starts)
    return jnp.transpose(per_head, (1, 0, 2)).reshape(sample_ids.shape[0], D)

def reference(query_rows, key_rows, value_rows, seg_ids, timesteps, w_mod):
    row_total = query_rows.shape[0]
    row_bins = (seg_ids // SEG_BIN).astype(jnp.int32)
    row_order = jnp.argsort(row_bins, stable=True).astype(jnp.int32)
    counts = lax.optimization_barrier(jnp.sum((row_bins[None, :] == jnp.arange(N_DP, dtype=jnp.int32)[:, None]).astype(jnp.int32), axis=1))
    starts = (jnp.cumsum(counts) - counts).astype(jnp.int32)
    order_padded = jnp.concatenate([row_order, jnp.full((BIN_SLOTS,), row_total, jnp.int32)])
    zero_row = jnp.zeros((1, D), jnp.bfloat16)
    query_padded = jnp.concatenate([query_rows, zero_row])
    key_padded = jnp.concatenate([key_rows, zero_row])
    value_padded = jnp.concatenate([value_rows, zero_row])
    ids_padded = jnp.concatenate([seg_ids, jnp.full((1,), -1, jnp.int32)])

    def one_bin(bin_number):
        picked = lax.dynamic_slice_in_dim(order_padded, starts[bin_number], BIN_SLOTS)
        live_slots = jnp.arange(BIN_SLOTS) < counts[bin_number]
        picked = jnp.where(live_slots, picked, row_total).astype(jnp.int32)
        attended = attend_bin(query_padded[picked], key_padded[picked], value_padded[picked], ids_padded[picked])
        return (picked, attended)
    picked_all, attended_all = lax.map(one_bin, jnp.arange(N_DP, dtype=jnp.int32))
    attended = jnp.zeros((row_total + 1, D), jnp.bfloat16)
    attended = attended.at[picked_all.reshape(-1)].set(attended_all.reshape(-1, D))[:row_total]
    scale_table = scale_rows_table(timesteps, w_mod)
    row_scales = scale_table[seg_ids]
    return (attended.astype(jnp.float32) * (1.0 + row_scales)).astype(jnp.bfloat16)
```

```python
import functools
import math

import jax
import jax.numpy as jnp
from jax import lax
from jax.experimental import pallas as pl
from jax.experimental.pallas import tpu as pltpu
from jax.sharding import PartitionSpec as P

HEAD_DIM = 128
FREQ = 256
SEG_BIN = 2


def for_sending(value):
    return jax.tree.map(lambda a: a.astype(jnp.bfloat16) if a.dtype == jnp.float32 else a, value)


def scale_rows_table(timesteps, w_mod):
    half_freq = FREQ // 2
    frequencies = jnp.exp(-math.log(10000.0) * jnp.arange(half_freq, dtype=jnp.float32) / half_freq)
    angles = timesteps.astype(jnp.float32)[:, None] * frequencies[None, :]
    embedding = jnp.concatenate([jnp.cos(angles), jnp.sin(angles)], axis=1)
    activated = jax.nn.silu(embedding).astype(jnp.bfloat16)
    return jnp.dot(activated, w_mod, preferred_element_type=jnp.float32)


def slot_places(row_bins, bin_count, capacity):
    bin_hits = (row_bins[:, None] == jnp.arange(bin_count, dtype=jnp.int32)[None, :]).astype(
        jnp.int32
    )
    ranks = jnp.cumsum(bin_hits, axis=0) - bin_hits
    slot_rank = jnp.sum(ranks * bin_hits, axis=1)
    target = row_bins * capacity + slot_rank
    return jnp.arange(bin_count * capacity, dtype=jnp.int32)[:, None] == target[None, :]


def slot_ids_of(placement, sample_ids):
    return jnp.sum(jnp.where(placement, sample_ids[None, :] + 1, 0), axis=1) - 1


def attend_slots(query_part, key_part, value_part, sample_ids):
    length, row_width = query_part.shape
    head_count = row_width // HEAD_DIM
    block_rows = min(512, length)
    score_scale = 1.0 / math.sqrt(HEAD_DIM)
    query_blocks = query_part.reshape(length // block_rows, block_rows, head_count, HEAD_DIM)
    key_heads = key_part.reshape(length, head_count, HEAD_DIM)
    value_heads = value_part.reshape(length, head_count, HEAD_DIM)
    id_blocks = sample_ids.reshape(length // block_rows, block_rows)

    def one_block(block_pair):
        query_block, query_ids = block_pair
        scores = (
            jnp.einsum("qhd,khd->hqk", query_block, key_heads, preferred_element_type=jnp.float32)
            * score_scale
        )
        same_sample = query_ids[:, None] == sample_ids[None, :]
        scores = jnp.where(same_sample[None], scores, -1e30)
        row_max = jnp.max(scores, axis=2, keepdims=True)
        weights = jnp.exp(scores - row_max)
        soft_probs = (weights / jnp.sum(weights, axis=2, keepdims=True)).astype(jnp.bfloat16)
        block_out = jnp.einsum(
            "hqk,khd->qhd", soft_probs, value_heads, preferred_element_type=jnp.float32
        )
        return block_out.astype(jnp.bfloat16).reshape(block_rows, row_width)

    return lax.map(one_block, (query_blocks, id_blocks)).reshape(length, row_width)


def place_rows(place_mask, arrays):
    return tuple(
        (
            jnp.dot(place_mask, single, preferred_element_type=jnp.float32).astype(jnp.bfloat16)
            for single in arrays
        )
    )


def routed_shards(query_rows, key_rows, value_rows, seg_ids, timesteps, w_mod):
    dp_count = lax.axis_size("dp")
    seq_count = lax.axis_size("seq")
    row_count = query_rows.shape[0]
    capacity = 2 * row_count // dp_count
    ids_tiled = jnp.broadcast_to(seg_ids[:, None], (row_count, seq_count))
    group_ids = lax.all_to_all(ids_tiled, "seq", split_axis=1, concat_axis=0, tiled=True).reshape(
        -1
    )
    head_parts = (
        lax.all_to_all(query_rows, "seq", split_axis=1, concat_axis=0, tiled=True),
        lax.all_to_all(key_rows, "seq", split_axis=1, concat_axis=0, tiled=True),
        lax.all_to_all(value_rows, "seq", split_axis=1, concat_axis=0, tiled=True),
    )
    placement = slot_places(group_ids // SEG_BIN, dp_count, seq_count * capacity)
    place_mask = placement.astype(jnp.bfloat16)
    slotted = place_rows(place_mask, head_parts)
    bin_ids = lax.all_to_all(
        slot_ids_of(placement, group_ids), "dp", split_axis=0, concat_axis=0, tiled=True
    )
    bin_query, bin_key, bin_value = jax.tree.map(
        lambda part, own: part.astype(own.dtype),
        lax.all_to_all(for_sending(slotted), "dp", split_axis=0, concat_axis=0, tiled=True),
        slotted,
    )
    attended = attend_slots(bin_query, bin_key, bin_value, bin_ids)
    returned = lax.all_to_all(attended, "dp", split_axis=0, concat_axis=0, tiled=True)
    unslotted = jnp.dot(place_mask.T, returned, preferred_element_type=jnp.float32).astype(
        jnp.bfloat16
    )
    home_rows = lax.all_to_all(unslotted, "seq", split_axis=0, concat_axis=1, tiled=True)
    scale_table = scale_rows_table(timesteps, w_mod)
    lookup = (
        seg_ids[:, None] == jnp.arange(scale_table.shape[0], dtype=jnp.int32)[None, :]
    ).astype(jnp.float32)
    row_scales = jnp.dot(
        lookup, scale_table, precision=lax.Precision.HIGHEST, preferred_element_type=jnp.float32
    )
    return (home_rows.astype(jnp.float32) * (1.0 + row_scales)).astype(jnp.bfloat16)


EXCLUDED = float(1 << 20)
NT = (((1,), (1,)), ((), ()))
TN = (((0,), (0,)), ((), ()))
QUARTERS = 4


def head_kernel(
    sizes,
    q_ref,
    k_ref,
    v_ref,
    ids_ref,
    times_ref,
    w_ref,
    out_ref,
    rows_buf,
    ids_buf,
    times_buf,
    w_buf,
    table_buf,
    place_buf,
    q_slots,
    k_slots,
    v_slots,
    group_out,
    out_buf,
    sem_send,
    sem_recv,
    sem_side,
    sweep,
    line,
):
    dp_count, seq_count, capacity = sizes
    count = dp_count * seq_count
    slab = count // QUARTERS
    row_count = out_ref.shape[0]
    slot_count = dp_count * capacity
    me = lax.axis_index("dp") * seq_count + lax.axis_index("seq")
    quarter = me // slab
    spot = me % slab
    inner = (quarter == 1) | (quarter == 2)
    outer = (quarter == 0) | (quarter == 3)
    partner = quarter + 1 - 2 * (quarter % 2)
    across = QUARTERS - 1 - quarter
    beyond = QUARTERS - 1 - partner
    sources = (k_ref, v_ref, q_ref)

    def device_of(index):
        return (index // seq_count, index % seq_count)

    def mixed_spot(step):
        total, bit = 0, 1
        while bit < slab:
            total = total + (spot // bit + step // bit) % 2 * bit
            bit *= 2
        return total

    def at_spot(of_quarter, step):
        return of_quarter * slab + mixed_spot(step)

    def head_columns(index):
        return pl.ds(pl.multiple_of(index * HEAD_DIM, HEAD_DIM), HEAD_DIM)

    def part_copy(part, target):
        return pltpu.make_async_remote_copy(
            src_ref=sources[part].at[:, head_columns(target)],
            dst_ref=rows_buf.at[part, me],
            send_sem=sem_send.at[part],
            recv_sem=sem_recv.at[part, quarter],
            device_id=device_of(target),
            device_id_type=pl.DeviceIdType.MESH,
        )

    def ids_copy(target):
        return pltpu.make_async_remote_copy(
            src_ref=ids_ref,
            dst_ref=ids_buf.at[me],
            send_sem=sem_send.at[3],
            recv_sem=sem_recv.at[3, quarter],
            device_id=device_of(target),
            device_id_type=pl.DeviceIdType.MESH,
        )

    def out_copy(target):
        return pltpu.make_async_remote_copy(
            src_ref=out_buf.at[target],
            dst_ref=out_ref.at[:, head_columns(me)],
            send_sem=sem_send.at[4],
            recv_sem=sem_side.at[0],
            device_id=device_of(target),
            device_id_type=pl.DeviceIdType.MESH,
        )

    def own_out():
        return pltpu.make_async_copy(
            out_buf.at[me], out_ref.at[:, head_columns(me)], sem_side.at[0]
        )

    def wait_for(region, sem):
        pltpu.make_async_copy(region, region, sem).wait()

    def slab_of(of_quarter):
        return pl.ds(pl.multiple_of(of_quarter * slab, slab), slab)

    def tell(sem, target):
        pl.semaphore_signal(
            sem, inc=1, device_id=device_of(target), device_id_type=pl.DeviceIdType.MESH
        )

    def send_k(target):
        ids_copy(target).start()
        part_copy(0, target).start()

    barrier = pltpu.get_barrier_semaphore()
    pair = min(2, slab)
    bits = [1 << n for n in range(slab.bit_length() - 1)]

    @pl.when(inner)
    def _():
        for step in range(pair):
            tell(barrier, at_spot(across, step))
        for step in range(pair):
            tell(barrier, at_spot(partner, step))

    for bit in bits:
        tell(barrier, at_spot(quarter, bit))

    for part in range(3):
        pltpu.make_async_copy(
            sources[part].at[:, head_columns(me)], rows_buf.at[part, me], sem_recv.at[part, quarter]
        ).start()
    pltpu.make_async_copy(ids_ref, ids_buf.at[me], sem_recv.at[3, quarter]).start()
    times_copy = pltpu.make_async_copy(times_ref, times_buf, sem_side.at[1])
    w_copy = pltpu.make_async_copy(w_ref.at[:, head_columns(me)], w_buf, sem_side.at[2])
    times_copy.start()
    w_copy.start()

    pl.semaphore_wait(barrier, len(bits) + pair)

    @pl.when(inner)
    def _():
        for step in range(pair):
            send_k(at_spot(across, step))

    for n, bit in enumerate(bits[1:]):
        tell(sweep.at[n], at_spot(quarter, bit))
        pl.semaphore_wait(sweep.at[n], 1)

    @pl.when(outer)
    def _():
        tell(line.at[0], at_spot(partner, 0))
        for step in range(1, slab):
            send_k(at_spot(quarter, step))
        for step in range(slab):
            send_k(at_spot(partner, step))
        pl.semaphore_wait(line.at[0], 1)
        for step in range(slab):
            send_k(at_spot(across, step))
            send_k(at_spot(beyond, step))

    @pl.when(inner)
    def _():
        for step in range(pair, slab):
            send_k(at_spot(across, step))
        pl.semaphore_wait(line.at[0], 1)
        tell(line.at[1], at_spot(across, 0))
        for step in range(1, slab):
            send_k(at_spot(quarter, step))
        pl.semaphore_wait(line.at[1], 1)
        tell(line.at[0], at_spot(partner, 0))
        for step in range(slab):
            send_k(at_spot(beyond, step))
            send_k(at_spot(partner, step))

    def send_part(part):
        @pl.loop(0, slab)
        def _(step):
            part_copy(part, at_spot(across, step)).start()
            part_copy(part, at_spot(beyond, step)).start()
            part_copy(part, at_spot(partner, step)).start()

            @pl.when(step > 0)
            def _():
                part_copy(part, at_spot(quarter, step)).start()

    send_part(1)
    send_part(2)

    times_copy.wait()
    samples = times_buf.shape[1]
    square = (samples, samples)
    diagonal = lax.broadcasted_iota(jnp.int32, square, 0) == lax.broadcasted_iota(
        jnp.int32, square, 1
    )
    times = jnp.broadcast_to(times_buf[...].astype(jnp.float32), square)
    times = jnp.sum(jnp.where(diagonal, times, 0.0), axis=1, keepdims=True)
    half_freq = FREQ // 2
    ramp = lax.broadcasted_iota(jnp.int32, (1, half_freq), 1).astype(jnp.float32)
    angles = times * jnp.exp(-math.log(10000.0) * ramp / half_freq)
    waves = (jax.nn.silu(wave(angles)).astype(jnp.bfloat16) for wave in (jnp.cos, jnp.sin))
    w_copy.wait()
    table_buf[...] = sum(
        jnp.dot(
            wave, w_buf[n * half_freq : (n + 1) * half_freq, :], preferred_element_type=jnp.float32
        )
        for n, wave in enumerate(waves)
    )

    v_slots[:, :, HEAD_DIM:] = jnp.ones((dp_count, count * capacity, HEAD_DIM), jnp.bfloat16)
    before = (
        lax.broadcasted_iota(jnp.int32, (row_count, row_count), 0)
        < lax.broadcasted_iota(jnp.int32, (row_count, row_count), 1)
    ).astype(jnp.bfloat16)
    part_lane = lax.broadcasted_iota(jnp.int32, (1, HEAD_DIM), 1) < SEG_BIN

    def member_hits(origin):
        ids = ids_buf[origin]
        member = ids - ids // SEG_BIN * SEG_BIN
        return lax.broadcasted_iota(jnp.int32, (HEAD_DIM, row_count), 0) == member

    def marks_of(place, hits):
        return lax.dot_general(
            place, hits.astype(jnp.bfloat16), NT, preferred_element_type=jnp.float32
        )

    def placed_part(place, origin, part):
        return jnp.dot(place, rows_buf[part, origin], preferred_element_type=jnp.float32)

    def by_bin(value):
        return value.astype(jnp.bfloat16).reshape((dp_count, capacity, HEAD_DIM))

    def slots_at(index):
        return pl.ds(pl.multiple_of(index * capacity, capacity), capacity)

    def place_k(origin):
        bins = ids_buf[origin] // SEG_BIN
        bin_hits = lax.broadcasted_iota(jnp.int32, (16, row_count), 0) == bins
        ranks = jnp.dot(
            bin_hits.astype(jnp.bfloat16), before, preferred_element_type=jnp.float32
        )
        rank = jnp.sum(jnp.where(bin_hits, ranks, 0.0), axis=0, keepdims=True)
        slot = bins * capacity + rank.astype(jnp.int32)
        place = (
            lax.broadcasted_iota(jnp.int32, (slot_count, row_count), 0) == slot
        ).astype(jnp.bfloat16)
        place_buf[origin] = place
        other_member = marks_of(place, jnp.logical_not(member_hits(origin)))
        k_marks = jnp.where(part_lane, 1.0 - other_member, 0.0)
        k_slots[:, slots_at(origin), :HEAD_DIM] = by_bin(placed_part(place, origin, 0))
        k_slots[:, slots_at(origin), HEAD_DIM:] = by_bin(k_marks)

    def place_v(origin):
        placed = placed_part(place_buf[origin], origin, 1)
        v_slots[:, slots_at(origin), :HEAD_DIM] = by_bin(placed)

    def place_q(origin, inner_index):
        place = place_buf[origin]
        own_member = marks_of(place, member_hits(origin))
        q_marks = jnp.where(part_lane, (own_member - 1.0) * EXCLUDED, 0.0)
        at = slice(inner_index * capacity, (inner_index + 1) * capacity)
        q_slots[:, at, :HEAD_DIM] = by_bin(placed_part(place, origin, 2))
        q_slots[:, at, HEAD_DIM:] = by_bin(q_marks)

    def arrived(part, of_quarter):
        wait_for(rows_buf.at[part, slab_of(of_quarter)], sem_recv.at[part, of_quarter])

    def turn_quarter(turn):
        near = jnp.where(turn == 0, quarter, partner)
        far = jnp.where(turn == 2, across, beyond)
        return jnp.where(turn < 2, near, far)

    @pl.loop(0, QUARTERS)
    def _(turn):
        of_quarter = turn_quarter(turn)
        wait_for(ids_buf.at[slab_of(of_quarter)], sem_recv.at[3, of_quarter])
        arrived(0, of_quarter)

        @pl.loop(0, slab)
        def _(n):
            place_k(of_quarter * slab + n)

    @pl.loop(0, QUARTERS)
    def _(turn):
        of_quarter = turn_quarter(turn)
        arrived(1, of_quarter)

        @pl.loop(0, slab)
        def _(n):
            place_v(of_quarter * slab + n)

    exponent_scale = 1.0 / (math.sqrt(HEAD_DIM) * math.log(2.0))
    group_slots = slab * capacity

    @pl.loop(0, QUARTERS)
    def _(turn):
        of_quarter = turn_quarter(turn)
        arrived(2, of_quarter)
        for n in range(slab):
            place_q(of_quarter * slab + n, n)

        @pl.loop(0, dp_count, unroll=8)
        def _(bin_index):
            query = q_slots[bin_index]
            scores = lax.dot_general(
                query, k_slots[bin_index], NT, preferred_element_type=jnp.float32
            )
            row_max = jnp.max(scores, axis=1, keepdims=True)
            weights = jnp.exp2((scores - row_max) * exponent_scale).astype(jnp.bfloat16)
            sums = jnp.dot(weights, v_slots[bin_index], preferred_element_type=jnp.float32)
            attended = (sums[:, :HEAD_DIM] / sums[:, HEAD_DIM:]).astype(jnp.bfloat16)
            factor = jnp.zeros((group_slots, HEAD_DIM), jnp.float32)
            for member in range(SEG_BIN):
                mark = query[:, HEAD_DIM + member : HEAD_DIM + member + 1].astype(jnp.float32)
                row = table_buf[pl.ds(bin_index * SEG_BIN + member, 1), :]
                factor = jnp.where(mark == 0.0, 1.0 + row, factor)
            mixed = (attended.astype(jnp.float32) * factor).astype(jnp.bfloat16)
            group_out[bin_index] = mixed

        for n in range(slab):
            target = of_quarter * slab + n
            slots = group_out[:, n * capacity : (n + 1) * capacity, :].reshape(
                (slot_count, HEAD_DIM)
            )
            out_buf[target] = lax.dot_general(
                place_buf[target], slots, TN, preferred_element_type=jnp.float32
            ).astype(jnp.bfloat16)

            @pl.when(target == me)
            def _():
                own_out().start()

            @pl.when(target != me)
            def _():
                out_copy(target).start()

    others = pl.ds(0, (count - 1) * HEAD_DIM)
    for part in range(3):
        wait_for(sources[part].at[:, others], sem_send.at[part])
    wait_for(ids_buf.at[pl.ds(0, count - 1)], sem_send.at[3])
    wait_for(out_buf.at[pl.ds(0, count - 1)], sem_send.at[4])
    wait_for(out_ref, sem_side.at[0])


def head_shards(query_rows, key_rows, value_rows, seg_ids, timesteps, w_mod):
    dp_count = lax.axis_size("dp")
    seq_count = lax.axis_size("seq")
    count = dp_count * seq_count
    row_count, width = query_rows.shape
    samples = timesteps.shape[0]
    capacity = 2 * row_count // dp_count
    slab = count // QUARTERS
    anywhere = pl.BlockSpec(memory_space=pl.ANY)
    slots = (dp_count, count * capacity, 2 * HEAD_DIM)
    return pl.pallas_call(
        functools.partial(head_kernel, (dp_count, seq_count, capacity)),
        out_shape=pltpu.VMEM((row_count, width), jnp.bfloat16),
        in_specs=[anywhere] * 6,
        out_specs=pl.BlockSpec(memory_space=pltpu.VMEM),
        scratch_shapes=[
            pltpu.VMEM((3, count, row_count, HEAD_DIM), jnp.bfloat16),
            pltpu.VMEM((count, 1, row_count), jnp.int32),
            pltpu.VMEM((1, samples), jnp.int32),
            pltpu.VMEM((FREQ, HEAD_DIM), jnp.bfloat16),
            pltpu.VMEM((samples, HEAD_DIM), jnp.float32),
            pltpu.VMEM((count, dp_count * capacity, row_count), jnp.bfloat16),
            pltpu.VMEM((dp_count, slab * capacity, 2 * HEAD_DIM), jnp.bfloat16),
            pltpu.VMEM(slots, jnp.bfloat16),
            pltpu.VMEM(slots, jnp.bfloat16),
            pltpu.VMEM((dp_count, slab * capacity, HEAD_DIM), jnp.bfloat16),
            pltpu.VMEM((count, row_count, HEAD_DIM), jnp.bfloat16),
            pltpu.SemaphoreType.DMA((5,)),
            pltpu.SemaphoreType.DMA((4, QUARTERS)),
            pltpu.SemaphoreType.DMA((3,)),
            pltpu.SemaphoreType.REGULAR((slab.bit_length(),)),
            pltpu.SemaphoreType.REGULAR((2,)),
        ],
        compiler_params=pltpu.CompilerParams(
            collective_id=0, has_side_effects=True, vmem_limit_bytes=56 * 1024 * 1024
        ),
    )(
        query_rows,
        key_rows,
        value_rows,
        seg_ids.reshape(1, row_count),
        timesteps.reshape(1, samples),
        w_mod,
    )


def shards(query_rows, key_rows, value_rows, seg_ids, timesteps, w_mod):
    count = lax.axis_size("dp") * lax.axis_size("seq")
    whole_heads = query_rows.shape[1] == count * HEAD_DIM
    slab = count // QUARTERS
    even_slabs = count == slab * QUARTERS and slab & (slab - 1) == 0 and slab > 1
    body = head_shards if whole_heads and even_slabs else routed_shards
    return body(query_rows, key_rows, value_rows, seg_ids, timesteps, w_mod)


def solution(mesh):
    placed = (
        P(("dp", "seq"), None),
        P(("dp", "seq"), None),
        P(("dp", "seq"), None),
        P(("dp", "seq")),
        P(),
        P(),
    )
    return jax.shard_map(
        shards, mesh=mesh, in_specs=placed, out_specs=P(("dp", "seq"), None), check_vma=False
    )
```

```python
import functools
import math

import jax
import jax.numpy as jnp
from jax import lax
from jax.experimental import pallas as pl
from jax.experimental.pallas import tpu as pltpu
from jax.sharding import PartitionSpec as P

HEAD_DIM = 128
FREQ = 256
SEG_BIN = 2


def for_sending(value):
    return jax.tree.map(lambda a: a.astype(jnp.bfloat16) if a.dtype == jnp.float32 else a, value)


def scale_rows_table(timesteps, w_mod):
    half_freq = FREQ // 2
    frequencies = jnp.exp(-math.log(10000.0) * jnp.arange(half_freq, dtype=jnp.float32) / half_freq)
    angles = timesteps.astype(jnp.float32)[:, None] * frequencies[None, :]
    embedding = jnp.concatenate([jnp.cos(angles), jnp.sin(angles)], axis=1)
    activated = jax.nn.silu(embedding).astype(jnp.bfloat16)
    return jnp.dot(activated, w_mod, preferred_element_type=jnp.float32)


def slot_places(row_bins, bin_count, capacity):
    bin_hits = (row_bins[:, None] == jnp.arange(bin_count, dtype=jnp.int32)[None, :]).astype(
        jnp.int32
    )
    ranks = jnp.cumsum(bin_hits, axis=0) - bin_hits
    slot_rank = jnp.sum(ranks * bin_hits, axis=1)
    target = row_bins * capacity + slot_rank
    return jnp.arange(bin_count * capacity, dtype=jnp.int32)[:, None] == target[None, :]


def slot_ids_of(placement, sample_ids):
    return jnp.sum(jnp.where(placement, sample_ids[None, :] + 1, 0), axis=1) - 1


def attend_slots(query_part, key_part, value_part, sample_ids):
    length, row_width = query_part.shape
    head_count = row_width // HEAD_DIM
    block_rows = min(512, length)
    score_scale = 1.0 / math.sqrt(HEAD_DIM)
    query_blocks = query_part.reshape(length // block_rows, block_rows, head_count, HEAD_DIM)
    key_heads = key_part.reshape(length, head_count, HEAD_DIM)
    value_heads = value_part.reshape(length, head_count, HEAD_DIM)
    id_blocks = sample_ids.reshape(length // block_rows, block_rows)

    def one_block(block_pair):
        query_block, query_ids = block_pair
        scores = (
            jnp.einsum("qhd,khd->hqk", query_block, key_heads, preferred_element_type=jnp.float32)
            * score_scale
        )
        same_sample = query_ids[:, None] == sample_ids[None, :]
        scores = jnp.where(same_sample[None], scores, -1e30)
        row_max = jnp.max(scores, axis=2, keepdims=True)
        weights = jnp.exp(scores - row_max)
        soft_probs = (weights / jnp.sum(weights, axis=2, keepdims=True)).astype(jnp.bfloat16)
        block_out = jnp.einsum(
            "hqk,khd->qhd", soft_probs, value_heads, preferred_element_type=jnp.float32
        )
        return block_out.astype(jnp.bfloat16).reshape(block_rows, row_width)

    return lax.map(one_block, (query_blocks, id_blocks)).reshape(length, row_width)


def place_rows(place_mask, arrays):
    return tuple(
        (
            jnp.dot(place_mask, single, preferred_element_type=jnp.float32).astype(jnp.bfloat16)
            for single in arrays
        )
    )


def routed_shards(query_rows, key_rows, value_rows, seg_ids, timesteps, w_mod):
    dp_count = lax.axis_size("dp")
    seq_count = lax.axis_size("seq")
    row_count = query_rows.shape[0]
    capacity = 2 * row_count // dp_count
    ids_tiled = jnp.broadcast_to(seg_ids[:, None], (row_count, seq_count))
    group_ids = lax.all_to_all(ids_tiled, "seq", split_axis=1, concat_axis=0, tiled=True).reshape(
        -1
    )
    head_parts = (
        lax.all_to_all(query_rows, "seq", split_axis=1, concat_axis=0, tiled=True),
        lax.all_to_all(key_rows, "seq", split_axis=1, concat_axis=0, tiled=True),
        lax.all_to_all(value_rows, "seq", split_axis=1, concat_axis=0, tiled=True),
    )
    placement = slot_places(group_ids // SEG_BIN, dp_count, seq_count * capacity)
    place_mask = placement.astype(jnp.bfloat16)
    slotted = place_rows(place_mask, head_parts)
    bin_ids = lax.all_to_all(
        slot_ids_of(placement, group_ids), "dp", split_axis=0, concat_axis=0, tiled=True
    )
    bin_query, bin_key, bin_value = jax.tree.map(
        lambda part, own: part.astype(own.dtype),
        lax.all_to_all(for_sending(slotted), "dp", split_axis=0, concat_axis=0, tiled=True),
        slotted,
    )
    attended = attend_slots(bin_query, bin_key, bin_value, bin_ids)
    returned = lax.all_to_all(attended, "dp", split_axis=0, concat_axis=0, tiled=True)
    unslotted = jnp.dot(place_mask.T, returned, preferred_element_type=jnp.float32).astype(
        jnp.bfloat16
    )
    home_rows = lax.all_to_all(unslotted, "seq", split_axis=0, concat_axis=1, tiled=True)
    scale_table = scale_rows_table(timesteps, w_mod)
    lookup = (
        seg_ids[:, None] == jnp.arange(scale_table.shape[0], dtype=jnp.int32)[None, :]
    ).astype(jnp.float32)
    row_scales = jnp.dot(
        lookup, scale_table, precision=lax.Precision.HIGHEST, preferred_element_type=jnp.float32
    )
    return (home_rows.astype(jnp.float32) * (1.0 + row_scales)).astype(jnp.bfloat16)


EXCLUDED = float(1 << 20)
NT = (((1,), (1,)), ((), ()))
TN = (((0,), (0,)), ((), ()))
QUARTERS = 4


def head_kernel(
    sizes,
    q_ref,
    k_ref,
    v_ref,
    ids_ref,
    times_ref,
    w_ref,
    out_ref,
    rows_buf,
    ids_buf,
    times_buf,
    w_buf,
    table_buf,
    place_buf,
    q_slots,
    k_slots,
    v_slots,
    group_out,
    out_buf,
    sem_send,
    sem_recv,
    sem_side,
    sweep,
    line,
):
    dp_count, seq_count, capacity = sizes
    count = dp_count * seq_count
    slab = count // QUARTERS
    row_count = out_ref.shape[0]
    slot_count = dp_count * capacity
    me = lax.axis_index("dp") * seq_count + lax.axis_index("seq")
    quarter = me // slab
    spot = me % slab
    inner = (quarter == 1) | (quarter == 2)
    outer = (quarter == 0) | (quarter == 3)
    partner = quarter + 1 - 2 * (quarter % 2)
    across = QUARTERS - 1 - quarter
    beyond = QUARTERS - 1 - partner
    sources = (k_ref, v_ref, q_ref)

    def device_of(index):
        return (index // seq_count, index % seq_count)

    def mixed_spot(step):
        total, bit = 0, 1
        while bit < slab:
            total = total + (spot // bit + step // bit) % 2 * bit
            bit *= 2
        return total

    def at_spot(of_quarter, step):
        return of_quarter * slab + mixed_spot(step)

    def head_columns(index):
        return pl.ds(pl.multiple_of(index * HEAD_DIM, HEAD_DIM), HEAD_DIM)

    def part_copy(part, target):
        return pltpu.make_async_remote_copy(
            src_ref=sources[part].at[:, head_columns(target)],
            dst_ref=rows_buf.at[part, me],
            send_sem=sem_send.at[part],
            recv_sem=sem_recv.at[part, quarter],
            device_id=device_of(target),
            device_id_type=pl.DeviceIdType.MESH,
        )

    def ids_copy(target):
        return pltpu.make_async_remote_copy(
            src_ref=ids_ref,
            dst_ref=ids_buf.at[me],
            send_sem=sem_send.at[3],
            recv_sem=sem_recv.at[3, quarter],
            device_id=device_of(target),
            device_id_type=pl.DeviceIdType.MESH,
        )

    def out_copy(target):
        return pltpu.make_async_remote_copy(
            src_ref=out_buf.at[target],
            dst_ref=out_ref.at[:, head_columns(me)],
            send_sem=sem_send.at[4],
            recv_sem=sem_side.at[0],
            device_id=device_of(target),
            device_id_type=pl.DeviceIdType.MESH,
        )

    def own_out():
        return pltpu.make_async_copy(
            out_buf.at[me], out_ref.at[:, head_columns(me)], sem_side.at[0]
        )

    def wait_for(region, sem):
        pltpu.make_async_copy(region, region, sem).wait()

    def slab_of(of_quarter):
        return pl.ds(pl.multiple_of(of_quarter * slab, slab), slab)

    def tell(sem, target):
        pl.semaphore_signal(
            sem, inc=1, device_id=device_of(target), device_id_type=pl.DeviceIdType.MESH
        )

    def send(part, target):
        if part == 0:
            ids_copy(target).start()
        part_copy(part, target).start()

    barrier = pltpu.get_barrier_semaphore()
    pair = min(2, slab)
    bits = [1 << n for n in range(slab.bit_length() - 1)]

    @pl.when(inner)
    def _():
        for step in range(pair):
            tell(barrier, at_spot(across, step))
        for step in range(pair):
            tell(barrier, at_spot(partner, step))

    for bit in bits:
        tell(barrier, at_spot(quarter, bit))

    for part in range(3):
        pltpu.make_async_copy(
            sources[part].at[:, head_columns(me)], rows_buf.at[part, me], sem_recv.at[part, quarter]
        ).start()
    pltpu.make_async_copy(ids_ref, ids_buf.at[me], sem_recv.at[3, quarter]).start()
    times_copy = pltpu.make_async_copy(times_ref, times_buf, sem_side.at[1])
    w_copy = pltpu.make_async_copy(w_ref.at[:, head_columns(me)], w_buf, sem_side.at[2])
    times_copy.start()
    w_copy.start()

    pl.semaphore_wait(barrier, len(bits) + pair)

    @pl.when(inner)
    def _():
        for part in range(2):
            for step in range(pair):
                send(part, at_spot(across, step))

    for n, bit in enumerate(bits[1:]):
        tell(sweep.at[n], at_spot(quarter, bit))
        pl.semaphore_wait(sweep.at[n], 1)

    def send_steps(part, of_quarter, first=0):
        @pl.loop(first, slab)
        def _(step):
            send(part, at_spot(of_quarter, step))

    @pl.when(outer)
    def _():
        tell(line.at[0], at_spot(partner, 0))

        for part in range(3):
            send(part, at_spot(partner, 0))

            @pl.loop(1, slab)
            def _(step):
                send(part, at_spot(partner, step))
                send(part, at_spot(quarter, step))

        pl.semaphore_wait(line.at[0], 1)

        for part in range(2):

            @pl.loop(0, slab)
            def _(step):
                send(part, at_spot(beyond, step))
                send(part, at_spot(across, step))

        send_steps(2, across)

    @pl.when(inner)
    def _():
        pl.semaphore_wait(line.at[0], 1)
        tell(line.at[1], at_spot(across, 0))
        for part in range(2):
            for step in range(pair):
                send(part, at_spot(partner, step))

            @pl.loop(pair, slab)
            def _(step):
                send(part, at_spot(across, step))
                send(part, at_spot(partner, step))

        pl.semaphore_wait(line.at[1], 1)
        tell(line.at[0], at_spot(partner, 0))
        for part in range(2):
            send(part, at_spot(beyond, 0))

            @pl.loop(1, slab)
            def _(step):
                send(part, at_spot(beyond, step))
                send(part, at_spot(quarter, step))

        send(2, at_spot(partner, 0))

        @pl.loop(1, slab)
        def _(step):
            send(2, at_spot(partner, step))
            send(2, at_spot(quarter, step))

    times_copy.wait()
    samples = times_buf.shape[1]
    square = (samples, samples)
    diagonal = lax.broadcasted_iota(jnp.int32, square, 0) == lax.broadcasted_iota(
        jnp.int32, square, 1
    )
    times = jnp.broadcast_to(times_buf[...].astype(jnp.float32), square)
    times = jnp.sum(jnp.where(diagonal, times, 0.0), axis=1, keepdims=True)
    half_freq = FREQ // 2
    ramp = lax.broadcasted_iota(jnp.int32, (1, half_freq), 1).astype(jnp.float32)
    angles = times * jnp.exp(-math.log(10000.0) * ramp / half_freq)
    waves = (jax.nn.silu(wave(angles)).astype(jnp.bfloat16) for wave in (jnp.cos, jnp.sin))
    w_copy.wait()
    table_buf[...] = sum(
        jnp.dot(
            wave, w_buf[n * half_freq : (n + 1) * half_freq, :], preferred_element_type=jnp.float32
        )
        for n, wave in enumerate(waves)
    )

    v_slots[:, :, HEAD_DIM:] = jnp.ones((dp_count, count * capacity, HEAD_DIM), jnp.bfloat16)
    before = (
        lax.broadcasted_iota(jnp.int32, (row_count, row_count), 0)
        < lax.broadcasted_iota(jnp.int32, (row_count, row_count), 1)
    ).astype(jnp.bfloat16)
    part_lane = lax.broadcasted_iota(jnp.int32, (1, HEAD_DIM), 1) < SEG_BIN

    def member_hits(origin):
        ids = ids_buf[origin]
        member = ids - ids // SEG_BIN * SEG_BIN
        return lax.broadcasted_iota(jnp.int32, (HEAD_DIM, row_count), 0) == member

    def marks_of(place, hits):
        return lax.dot_general(
            place, hits.astype(jnp.bfloat16), NT, preferred_element_type=jnp.float32
        )

    def placed_part(place, origin, part):
        return jnp.dot(place, rows_buf[part, origin], preferred_element_type=jnp.float32)

    def by_bin(value):
        return value.astype(jnp.bfloat16).reshape((dp_count, capacity, HEAD_DIM))

    def slots_at(index):
        return pl.ds(pl.multiple_of(index * capacity, capacity), capacity)

    def place_k(origin):
        bins = ids_buf[origin] // SEG_BIN
        bin_hits = lax.broadcasted_iota(jnp.int32, (16, row_count), 0) == bins
        ranks = jnp.dot(
            bin_hits.astype(jnp.bfloat16), before, preferred_element_type=jnp.float32
        )
        rank = jnp.sum(jnp.where(bin_hits, ranks, 0.0), axis=0, keepdims=True)
        slot = bins * capacity + rank.astype(jnp.int32)
        place = (
            lax.broadcasted_iota(jnp.int32, (slot_count, row_count), 0) == slot
        ).astype(jnp.bfloat16)
        place_buf[origin] = place
        other_member = marks_of(place, jnp.logical_not(member_hits(origin)))
        k_marks = jnp.where(part_lane, 1.0 - other_member, 0.0)
        k_slots[:, slots_at(origin), :HEAD_DIM] = by_bin(placed_part(place, origin, 0))
        k_slots[:, slots_at(origin), HEAD_DIM:] = by_bin(k_marks)

    def place_v(origin):
        placed = placed_part(place_buf[origin], origin, 1)
        v_slots[:, slots_at(origin), :HEAD_DIM] = by_bin(placed)

    def place_q(origin, inner_index):
        place = place_buf[origin]
        own_member = marks_of(place, member_hits(origin))
        q_marks = jnp.where(part_lane, (own_member - 1.0) * EXCLUDED, 0.0)
        at = slice(inner_index * capacity, (inner_index + 1) * capacity)
        q_slots[:, at, :HEAD_DIM] = by_bin(placed_part(place, origin, 2))
        q_slots[:, at, HEAD_DIM:] = by_bin(q_marks)

    def arrived(part, of_quarter):
        wait_for(rows_buf.at[part, slab_of(of_quarter)], sem_recv.at[part, of_quarter])

    def turn_quarter(turn, order):
        found = order[-1]
        for n in range(len(order) - 1):
            found = jnp.where(turn == n, order[n], found)
        return found

    far_inner = jnp.where(inner, across, beyond)
    far_outer = jnp.where(inner, beyond, across)
    arrivals = (quarter, partner, far_inner, far_outer)
    queries = (partner, quarter, across, beyond)

    @pl.loop(0, QUARTERS)
    def _(turn):
        of_quarter = turn_quarter(turn, arrivals)
        wait_for(ids_buf.at[slab_of(of_quarter)], sem_recv.at[3, of_quarter])
        arrived(0, of_quarter)

        @pl.loop(0, slab)
        def _(n):
            place_k(of_quarter * slab + n)

    @pl.loop(0, QUARTERS)
    def _(turn):
        of_quarter = turn_quarter(turn, arrivals)
        arrived(1, of_quarter)

        @pl.loop(0, slab)
        def _(n):
            place_v(of_quarter * slab + n)

    @pl.when(inner)
    def _():
        send_steps(2, across)
        send_steps(2, beyond)

    exponent_scale = 1.0 / (math.sqrt(HEAD_DIM) * math.log(2.0))
    group_slots = slab * capacity

    @pl.loop(0, QUARTERS)
    def _(turn):
        of_quarter = turn_quarter(turn, queries)
        arrived(2, of_quarter)
        for n in range(slab):
            place_q(of_quarter * slab + n, n)

        @pl.loop(0, dp_count, unroll=8)
        def _(bin_index):
            query = q_slots[bin_index]
            scores = lax.dot_general(
                query, k_slots[bin_index], NT, preferred_element_type=jnp.float32
            )
            row_max = jnp.max(scores, axis=1, keepdims=True)
            weights = jnp.exp2((scores - row_max) * exponent_scale).astype(jnp.bfloat16)
            sums = jnp.dot(weights, v_slots[bin_index], preferred_element_type=jnp.float32)
            attended = (sums[:, :HEAD_DIM] / sums[:, HEAD_DIM:]).astype(jnp.bfloat16)
            factor = jnp.zeros((group_slots, HEAD_DIM), jnp.float32)
            for member in range(SEG_BIN):
                mark = query[:, HEAD_DIM + member : HEAD_DIM + member + 1].astype(jnp.float32)
                row = table_buf[pl.ds(bin_index * SEG_BIN + member, 1), :]
                factor = jnp.where(mark == 0.0, 1.0 + row, factor)
            mixed = (attended.astype(jnp.float32) * factor).astype(jnp.bfloat16)
            group_out[bin_index] = mixed

        for n in range(slab):
            target = of_quarter * slab + n
            slots = group_out[:, n * capacity : (n + 1) * capacity, :].reshape(
                (slot_count, HEAD_DIM)
            )
            out_buf[target] = lax.dot_general(
                place_buf[target], slots, TN, preferred_element_type=jnp.float32
            ).astype(jnp.bfloat16)

            @pl.when(target == me)
            def _():
                own_out().start()

            @pl.when(target != me)
            def _():
                out_copy(target).start()

        @pl.when(outer & (turn == 0))
        def _():
            send_steps(2, beyond)

    others = pl.ds(0, (count - 1) * HEAD_DIM)
    for part in range(3):
        wait_for(sources[part].at[:, others], sem_send.at[part])
    wait_for(ids_buf.at[pl.ds(0, count - 1)], sem_send.at[3])
    wait_for(out_buf.at[pl.ds(0, count - 1)], sem_send.at[4])
    wait_for(out_ref, sem_side.at[0])


def head_shards(query_rows, key_rows, value_rows, seg_ids, timesteps, w_mod):
    dp_count = lax.axis_size("dp")
    seq_count = lax.axis_size("seq")
    count = dp_count * seq_count
    row_count, width = query_rows.shape
    samples = timesteps.shape[0]
    capacity = 2 * row_count // dp_count
    slab = count // QUARTERS
    anywhere = pl.BlockSpec(memory_space=pl.ANY)
    slots = (dp_count, count * capacity, 2 * HEAD_DIM)
    return pl.pallas_call(
        functools.partial(head_kernel, (dp_count, seq_count, capacity)),
        out_shape=pltpu.VMEM((row_count, width), jnp.bfloat16),
        in_specs=[anywhere] * 6,
        out_specs=pl.BlockSpec(memory_space=pltpu.VMEM),
        scratch_shapes=[
            pltpu.VMEM((3, count, row_count, HEAD_DIM), jnp.bfloat16),
            pltpu.VMEM((count, 1, row_count), jnp.int32),
            pltpu.VMEM((1, samples), jnp.int32),
            pltpu.VMEM((FREQ, HEAD_DIM), jnp.bfloat16),
            pltpu.VMEM((samples, HEAD_DIM), jnp.float32),
            pltpu.VMEM((count, dp_count * capacity, row_count), jnp.bfloat16),
            pltpu.VMEM((dp_count, slab * capacity, 2 * HEAD_DIM), jnp.bfloat16),
            pltpu.VMEM(slots, jnp.bfloat16),
            pltpu.VMEM(slots, jnp.bfloat16),
            pltpu.VMEM((dp_count, slab * capacity, HEAD_DIM), jnp.bfloat16),
            pltpu.VMEM((count, row_count, HEAD_DIM), jnp.bfloat16),
            pltpu.SemaphoreType.DMA((5,)),
            pltpu.SemaphoreType.DMA((4, QUARTERS)),
            pltpu.SemaphoreType.DMA((3,)),
            pltpu.SemaphoreType.REGULAR((slab.bit_length(),)),
            pltpu.SemaphoreType.REGULAR((2,)),
        ],
        compiler_params=pltpu.CompilerParams(
            collective_id=0, has_side_effects=True, vmem_limit_bytes=56 * 1024 * 1024
        ),
    )(
        query_rows,
        key_rows,
        value_rows,
        seg_ids.reshape(1, row_count),
        timesteps.reshape(1, samples),
        w_mod,
    )


def shards(query_rows, key_rows, value_rows, seg_ids, timesteps, w_mod):
    count = lax.axis_size("dp") * lax.axis_size("seq")
    whole_heads = query_rows.shape[1] == count * HEAD_DIM
    slab = count // QUARTERS
    even_slabs = count == slab * QUARTERS and slab & (slab - 1) == 0 and slab > 1
    body = head_shards if whole_heads and even_slabs else routed_shards
    return body(query_rows, key_rows, value_rows, seg_ids, timesteps, w_mod)


def solution(mesh):
    placed = (
        P(("dp", "seq"), None),
        P(("dp", "seq"), None),
        P(("dp", "seq"), None),
        P(("dp", "seq")),
        P(),
        P(),
    )
    return jax.shard_map(
        shards, mesh=mesh, in_specs=placed, out_specs=P(("dp", "seq"), None), check_vma=False
    )
```

```python
import functools
import math

import jax
import jax.numpy as jnp
from jax import lax
from jax.experimental import pallas as pl
from jax.experimental.pallas import tpu as pltpu
from jax.sharding import PartitionSpec as P

HEAD_DIM = 128
FREQ = 256
SEG_BIN = 2


def for_sending(value):
    return jax.tree.map(lambda a: a.astype(jnp.bfloat16) if a.dtype == jnp.float32 else a, value)


def scale_rows_table(timesteps, w_mod):
    half_freq = FREQ // 2
    frequencies = jnp.exp(-math.log(10000.0) * jnp.arange(half_freq, dtype=jnp.float32) / half_freq)
    angles = timesteps.astype(jnp.float32)[:, None] * frequencies[None, :]
    embedding = jnp.concatenate([jnp.cos(angles), jnp.sin(angles)], axis=1)
    activated = jax.nn.silu(embedding).astype(jnp.bfloat16)
    return jnp.dot(activated, w_mod, preferred_element_type=jnp.float32)


def slot_places(row_bins, bin_count, capacity):
    bin_hits = (row_bins[:, None] == jnp.arange(bin_count, dtype=jnp.int32)[None, :]).astype(
        jnp.int32
    )
    ranks = jnp.cumsum(bin_hits, axis=0) - bin_hits
    slot_rank = jnp.sum(ranks * bin_hits, axis=1)
    target = row_bins * capacity + slot_rank
    return jnp.arange(bin_count * capacity, dtype=jnp.int32)[:, None] == target[None, :]


def slot_ids_of(placement, sample_ids):
    return jnp.sum(jnp.where(placement, sample_ids[None, :] + 1, 0), axis=1) - 1


def attend_slots(query_part, key_part, value_part, sample_ids):
    length, row_width = query_part.shape
    head_count = row_width // HEAD_DIM
    block_rows = min(512, length)
    score_scale = 1.0 / math.sqrt(HEAD_DIM)
    query_blocks = query_part.reshape(length // block_rows, block_rows, head_count, HEAD_DIM)
    key_heads = key_part.reshape(length, head_count, HEAD_DIM)
    value_heads = value_part.reshape(length, head_count, HEAD_DIM)
    id_blocks = sample_ids.reshape(length // block_rows, block_rows)

    def one_block(block_pair):
        query_block, query_ids = block_pair
        scores = (
            jnp.einsum("qhd,khd->hqk", query_block, key_heads, preferred_element_type=jnp.float32)
            * score_scale
        )
        same_sample = query_ids[:, None] == sample_ids[None, :]
        scores = jnp.where(same_sample[None], scores, -1e30)
        row_max = jnp.max(scores, axis=2, keepdims=True)
        weights = jnp.exp(scores - row_max)
        soft_probs = (weights / jnp.sum(weights, axis=2, keepdims=True)).astype(jnp.bfloat16)
        block_out = jnp.einsum(
            "hqk,khd->qhd", soft_probs, value_heads, preferred_element_type=jnp.float32
        )
        return block_out.astype(jnp.bfloat16).reshape(block_rows, row_width)

    return lax.map(one_block, (query_blocks, id_blocks)).reshape(length, row_width)


def place_rows(place_mask, arrays):
    return tuple(
        (
            jnp.dot(place_mask, single, preferred_element_type=jnp.float32).astype(jnp.bfloat16)
            for single in arrays
        )
    )


def routed_shards(query_rows, key_rows, value_rows, seg_ids, timesteps, w_mod):
    dp_count = lax.axis_size("dp")
    seq_count = lax.axis_size("seq")
    row_count = query_rows.shape[0]
    capacity = 2 * row_count // dp_count
    ids_tiled = jnp.broadcast_to(seg_ids[:, None], (row_count, seq_count))
    group_ids = lax.all_to_all(ids_tiled, "seq", split_axis=1, concat_axis=0, tiled=True).reshape(
        -1
    )
    head_parts = (
        lax.all_to_all(query_rows, "seq", split_axis=1, concat_axis=0, tiled=True),
        lax.all_to_all(key_rows, "seq", split_axis=1, concat_axis=0, tiled=True),
        lax.all_to_all(value_rows, "seq", split_axis=1, concat_axis=0, tiled=True),
    )
    placement = slot_places(group_ids // SEG_BIN, dp_count, seq_count * capacity)
    place_mask = placement.astype(jnp.bfloat16)
    slotted = place_rows(place_mask, head_parts)
    bin_ids = lax.all_to_all(
        slot_ids_of(placement, group_ids), "dp", split_axis=0, concat_axis=0, tiled=True
    )
    bin_query, bin_key, bin_value = jax.tree.map(
        lambda part, own: part.astype(own.dtype),
        lax.all_to_all(for_sending(slotted), "dp", split_axis=0, concat_axis=0, tiled=True),
        slotted,
    )
    attended = attend_slots(bin_query, bin_key, bin_value, bin_ids)
    returned = lax.all_to_all(attended, "dp", split_axis=0, concat_axis=0, tiled=True)
    unslotted = jnp.dot(place_mask.T, returned, preferred_element_type=jnp.float32).astype(
        jnp.bfloat16
    )
    home_rows = lax.all_to_all(unslotted, "seq", split_axis=0, concat_axis=1, tiled=True)
    scale_table = scale_rows_table(timesteps, w_mod)
    lookup = (
        seg_ids[:, None] == jnp.arange(scale_table.shape[0], dtype=jnp.int32)[None, :]
    ).astype(jnp.float32)
    row_scales = jnp.dot(
        lookup, scale_table, precision=lax.Precision.HIGHEST, preferred_element_type=jnp.float32
    )
    return (home_rows.astype(jnp.float32) * (1.0 + row_scales)).astype(jnp.bfloat16)


EXCLUDED = float(1 << 20)
NT = (((1,), (1,)), ((), ()))
TN = (((0,), (0,)), ((), ()))
QUARTERS = 4


def head_kernel(
    sizes,
    q_ref,
    k_ref,
    v_ref,
    ids_ref,
    times_ref,
    w_ref,
    out_ref,
    rows_buf,
    ids_buf,
    times_buf,
    w_buf,
    table_buf,
    place_buf,
    q_slots,
    k_slots,
    v_slots,
    group_out,
    out_buf,
    sem_send,
    sem_recv,
    sem_side,
    sweep,
    line,
):
    dp_count, seq_count, capacity = sizes
    count = dp_count * seq_count
    slab = count // QUARTERS
    row_count = out_ref.shape[0]
    slot_count = dp_count * capacity
    me = lax.axis_index("dp") * seq_count + lax.axis_index("seq")
    quarter = me // slab
    spot = me % slab
    inner = (quarter == 1) | (quarter == 2)
    outer = (quarter == 0) | (quarter == 3)
    partner = quarter + 1 - 2 * (quarter % 2)
    across = QUARTERS - 1 - quarter
    beyond = QUARTERS - 1 - partner
    sources = (k_ref, v_ref, q_ref)

    def device_of(index):
        return (index // seq_count, index % seq_count)

    def mixed_spot(step):
        total, bit = 0, 1
        while bit < slab:
            total = total + (spot // bit + step // bit) % 2 * bit
            bit *= 2
        return total

    def at_spot(of_quarter, step):
        return of_quarter * slab + mixed_spot(step)

    def head_columns(index):
        return pl.ds(pl.multiple_of(index * HEAD_DIM, HEAD_DIM), HEAD_DIM)

    def part_copy(part, target):
        return pltpu.make_async_remote_copy(
            src_ref=sources[part].at[:, head_columns(target)],
            dst_ref=rows_buf.at[part, me],
            send_sem=sem_send.at[part],
            recv_sem=sem_recv.at[part, quarter],
            device_id=device_of(target),
            device_id_type=pl.DeviceIdType.MESH,
        )

    def ids_copy(target):
        return pltpu.make_async_remote_copy(
            src_ref=ids_ref,
            dst_ref=ids_buf.at[me],
            send_sem=sem_send.at[3],
            recv_sem=sem_recv.at[3, quarter],
            device_id=device_of(target),
            device_id_type=pl.DeviceIdType.MESH,
        )

    def out_copy(target):
        return pltpu.make_async_remote_copy(
            src_ref=out_buf.at[target],
            dst_ref=out_ref.at[:, head_columns(me)],
            send_sem=sem_send.at[4],
            recv_sem=sem_side.at[0],
            device_id=device_of(target),
            device_id_type=pl.DeviceIdType.MESH,
        )

    def own_out():
        return pltpu.make_async_copy(
            out_buf.at[me], out_ref.at[:, head_columns(me)], sem_side.at[0]
        )

    def wait_for(region, sem):
        pltpu.make_async_copy(region, region, sem).wait()

    def slab_of(of_quarter):
        return pl.ds(pl.multiple_of(of_quarter * slab, slab), slab)

    def tell(sem, target):
        pl.semaphore_signal(
            sem, inc=1, device_id=device_of(target), device_id_type=pl.DeviceIdType.MESH
        )

    def send(part, target):
        if part == 0:
            ids_copy(target).start()
        part_copy(part, target).start()

    barrier = pltpu.get_barrier_semaphore()
    pair = min(2, slab)
    bits = [1 << n for n in range(slab.bit_length() - 1)]

    @pl.when(inner)
    def _():
        for step in range(pair):
            tell(barrier, at_spot(across, step))
        for step in range(pair):
            tell(barrier, at_spot(partner, step))

    for bit in bits:
        tell(barrier, at_spot(quarter, bit))

    for part in range(3):
        pltpu.make_async_copy(
            sources[part].at[:, head_columns(me)], rows_buf.at[part, me], sem_recv.at[part, quarter]
        ).start()
    pltpu.make_async_copy(ids_ref, ids_buf.at[me], sem_recv.at[3, quarter]).start()
    times_copy = pltpu.make_async_copy(times_ref, times_buf, sem_side.at[1])
    w_copy = pltpu.make_async_copy(w_ref.at[:, head_columns(me)], w_buf, sem_side.at[2])
    times_copy.start()
    w_copy.start()

    pl.semaphore_wait(barrier, len(bits) + pair)

    @pl.when(inner)
    def _():
        for part in range(2):
            for step in range(pair):
                send(part, at_spot(across, step))

    for n, bit in enumerate(bits[1:]):
        tell(sweep.at[n], at_spot(quarter, bit))
        pl.semaphore_wait(sweep.at[n], 1)

    def send_rounds(*streams):
        @pl.loop(0, slab)
        def _(step):
            for part, of_quarter in streams:
                if of_quarter is quarter:
                    first = 1
                elif of_quarter is across and part < 2:
                    first = jnp.where(inner, pair, 0)
                else:
                    first = 0

                @pl.when(step >= first)
                def _():
                    send(part, at_spot(of_quarter, step))

    @pl.when(outer)
    def _():
        tell(line.at[0], at_spot(partner, 0))
        send_rounds((0, partner), (0, quarter))
        send_rounds((1, partner), (1, quarter))
        send_rounds((2, partner), (2, quarter))
        pl.semaphore_wait(line.at[0], 1)
        send_rounds((0, beyond), (0, across))
        send_rounds((1, beyond), (1, across))
        send_rounds((2, across))
        send_rounds((2, beyond))

    @pl.when(inner)
    def _():
        pl.semaphore_wait(line.at[0], 1)
        tell(line.at[1], at_spot(across, 0))
        send_rounds((0, across), (0, partner))
        send_rounds((1, across), (1, partner))
        pl.semaphore_wait(line.at[1], 1)
        tell(line.at[0], at_spot(partner, 0))
        send_rounds((0, beyond), (0, quarter))
        send_rounds((1, beyond), (1, quarter))
        send_rounds((2, partner), (2, quarter))

    times_copy.wait()
    samples = times_buf.shape[1]
    square = (samples, samples)
    diagonal = lax.broadcasted_iota(jnp.int32, square, 0) == lax.broadcasted_iota(
        jnp.int32, square, 1
    )
    times = jnp.broadcast_to(times_buf[...].astype(jnp.float32), square)
    times = jnp.sum(jnp.where(diagonal, times, 0.0), axis=1, keepdims=True)
    half_freq = FREQ // 2
    ramp = lax.broadcasted_iota(jnp.int32, (1, half_freq), 1).astype(jnp.float32)
    angles = times * jnp.exp(-math.log(10000.0) * ramp / half_freq)
    waves = (jax.nn.silu(wave(angles)).astype(jnp.bfloat16) for wave in (jnp.cos, jnp.sin))
    w_copy.wait()
    table_buf[...] = sum(
        jnp.dot(
            wave, w_buf[n * half_freq : (n + 1) * half_freq, :], preferred_element_type=jnp.float32
        )
        for n, wave in enumerate(waves)
    )

    v_slots[:, :, HEAD_DIM:] = jnp.ones((dp_count, count * capacity, HEAD_DIM), jnp.bfloat16)
    before = (
        lax.broadcasted_iota(jnp.int32, (row_count, row_count), 0)
        < lax.broadcasted_iota(jnp.int32, (row_count, row_count), 1)
    ).astype(jnp.bfloat16)
    part_lane = lax.broadcasted_iota(jnp.int32, (1, HEAD_DIM), 1) < SEG_BIN

    def member_hits(origin):
        ids = ids_buf[origin]
        member = ids - ids // SEG_BIN * SEG_BIN
        return lax.broadcasted_iota(jnp.int32, (HEAD_DIM, row_count), 0) == member

    def marks_of(place, hits):
        return lax.dot_general(
            place, hits.astype(jnp.bfloat16), NT, preferred_element_type=jnp.float32
        )

    def placed_part(place, origin, part):
        return jnp.dot(place, rows_buf[part, origin], preferred_element_type=jnp.float32)

    def by_bin(value):
        return value.astype(jnp.bfloat16).reshape((dp_count, capacity, HEAD_DIM))

    def slots_at(index):
        return pl.ds(pl.multiple_of(index * capacity, capacity), capacity)

    def place_k(origin):
        bins = ids_buf[origin] // SEG_BIN
        bin_hits = lax.broadcasted_iota(jnp.int32, (16, row_count), 0) == bins
        ranks = jnp.dot(
            bin_hits.astype(jnp.bfloat16), before, preferred_element_type=jnp.float32
        )
        rank = jnp.sum(jnp.where(bin_hits, ranks, 0.0), axis=0, keepdims=True)
        slot = bins * capacity + rank.astype(jnp.int32)
        place = (
            lax.broadcasted_iota(jnp.int32, (slot_count, row_count), 0) == slot
        ).astype(jnp.bfloat16)
        place_buf[origin] = place
        other_member = marks_of(place, jnp.logical_not(member_hits(origin)))
        k_marks = jnp.where(part_lane, 1.0 - other_member, 0.0)
        k_slots[:, slots_at(origin), :HEAD_DIM] = by_bin(placed_part(place, origin, 0))
        k_slots[:, slots_at(origin), HEAD_DIM:] = by_bin(k_marks)

    def place_v(origin):
        placed = placed_part(place_buf[origin], origin, 1)
        v_slots[:, slots_at(origin), :HEAD_DIM] = by_bin(placed)

    def place_q(origin, inner_index):
        place = place_buf[origin]
        own_member = marks_of(place, member_hits(origin))
        q_marks = jnp.where(part_lane, (own_member - 1.0) * EXCLUDED, 0.0)
        at = slice(inner_index * capacity, (inner_index + 1) * capacity)
        q_slots[:, at, :HEAD_DIM] = by_bin(placed_part(place, origin, 2))
        q_slots[:, at, HEAD_DIM:] = by_bin(q_marks)

    def arrived(part, of_quarter):
        wait_for(rows_buf.at[part, slab_of(of_quarter)], sem_recv.at[part, of_quarter])

    def turn_quarter(turn, order):
        found = order[-1]
        for n in range(len(order) - 1):
            found = jnp.where(turn == n, order[n], found)
        return found

    arrivals = (
        partner,
        jnp.where(inner, across, quarter),
        jnp.where(inner, quarter, beyond),
        jnp.where(inner, beyond, across),
    )
    queries = (
        partner,
        jnp.where(inner, beyond, across),
        quarter,
        jnp.where(inner, across, beyond),
    )

    @pl.loop(0, 2)
    def _(stage):
        @pl.loop(2 * stage, 2 * stage + 2)
        def _(turn):
            of_quarter = turn_quarter(turn, arrivals)
            wait_for(ids_buf.at[slab_of(of_quarter)], sem_recv.at[3, of_quarter])
            arrived(0, of_quarter)

            @pl.loop(0, slab)
            def _(n):
                place_k(of_quarter * slab + n)

        @pl.loop(2 * stage, 2 * stage + 2)
        def _(turn):
            of_quarter = turn_quarter(turn, arrivals)
            arrived(1, of_quarter)

            @pl.loop(0, slab)
            def _(n):
                place_v(of_quarter * slab + n)

    @pl.when(inner)
    def _():
        send_rounds((2, beyond))

    exponent_scale = 1.0 / (math.sqrt(HEAD_DIM) * math.log(2.0))
    group_slots = slab * capacity

    @pl.loop(0, QUARTERS)
    def _(turn):
        of_quarter = turn_quarter(turn, queries)
        arrived(2, of_quarter)

        @pl.when(inner & (turn == 1))
        def _():
            send_rounds((2, across))

        for n in range(slab):
            place_q(at_spot(of_quarter, n), n)

        @pl.loop(0, dp_count, unroll=8)
        def _(bin_index):
            query = q_slots[bin_index]
            scores = lax.dot_general(
                query, k_slots[bin_index], NT, preferred_element_type=jnp.float32
            )
            row_max = jnp.max(scores, axis=1, keepdims=True)
            weights = jnp.exp2((scores - row_max) * exponent_scale).astype(jnp.bfloat16)
            sums = jnp.dot(weights, v_slots[bin_index], preferred_element_type=jnp.float32)
            attended = (sums[:, :HEAD_DIM] / sums[:, HEAD_DIM:]).astype(jnp.bfloat16)
            factor = jnp.zeros((group_slots, HEAD_DIM), jnp.float32)
            for member in range(SEG_BIN):
                mark = query[:, HEAD_DIM + member : HEAD_DIM + member + 1].astype(jnp.float32)
                row = table_buf[pl.ds(bin_index * SEG_BIN + member, 1), :]
                factor = jnp.where(mark == 0.0, 1.0 + row, factor)
            mixed = (attended.astype(jnp.float32) * factor).astype(jnp.bfloat16)
            group_out[bin_index] = mixed

        for n in range(slab):
            target = at_spot(of_quarter, n)
            slots = group_out[:, n * capacity : (n + 1) * capacity, :].reshape(
                (slot_count, HEAD_DIM)
            )
            out_buf[target] = lax.dot_general(
                place_buf[target], slots, TN, preferred_element_type=jnp.float32
            ).astype(jnp.bfloat16)

            @pl.when(target == me)
            def _():
                own_out().start()

            @pl.when(target != me)
            def _():
                out_copy(target).start()

    others = pl.ds(0, (count - 1) * HEAD_DIM)
    for part in range(3):
        wait_for(sources[part].at[:, others], sem_send.at[part])
    wait_for(ids_buf.at[pl.ds(0, count - 1)], sem_send.at[3])
    wait_for(out_buf.at[pl.ds(0, count - 1)], sem_send.at[4])
    wait_for(out_ref, sem_side.at[0])


def head_shards(query_rows, key_rows, value_rows, seg_ids, timesteps, w_mod):
    dp_count = lax.axis_size("dp")
    seq_count = lax.axis_size("seq")
    count = dp_count * seq_count
    row_count, width = query_rows.shape
    samples = timesteps.shape[0]
    capacity = 2 * row_count // dp_count
    slab = count // QUARTERS
    anywhere = pl.BlockSpec(memory_space=pl.ANY)
    slots = (dp_count, count * capacity, 2 * HEAD_DIM)
    return pl.pallas_call(
        functools.partial(head_kernel, (dp_count, seq_count, capacity)),
        out_shape=pltpu.VMEM((row_count, width), jnp.bfloat16),
        in_specs=[anywhere] * 6,
        out_specs=pl.BlockSpec(memory_space=pltpu.VMEM),
        scratch_shapes=[
            pltpu.VMEM((3, count, row_count, HEAD_DIM), jnp.bfloat16),
            pltpu.VMEM((count, 1, row_count), jnp.int32),
            pltpu.VMEM((1, samples), jnp.int32),
            pltpu.VMEM((FREQ, HEAD_DIM), jnp.bfloat16),
            pltpu.VMEM((samples, HEAD_DIM), jnp.float32),
            pltpu.VMEM((count, dp_count * capacity, row_count), jnp.bfloat16),
            pltpu.VMEM((dp_count, slab * capacity, 2 * HEAD_DIM), jnp.bfloat16),
            pltpu.VMEM(slots, jnp.bfloat16),
            pltpu.VMEM(slots, jnp.bfloat16),
            pltpu.VMEM((dp_count, slab * capacity, HEAD_DIM), jnp.bfloat16),
            pltpu.VMEM((count, row_count, HEAD_DIM), jnp.bfloat16),
            pltpu.SemaphoreType.DMA((5,)),
            pltpu.SemaphoreType.DMA((4, QUARTERS)),
            pltpu.SemaphoreType.DMA((3,)),
            pltpu.SemaphoreType.REGULAR((slab.bit_length(),)),
            pltpu.SemaphoreType.REGULAR((2,)),
        ],
        compiler_params=pltpu.CompilerParams(
            collective_id=0, has_side_effects=True, vmem_limit_bytes=56 * 1024 * 1024
        ),
    )(
        query_rows,
        key_rows,
        value_rows,
        seg_ids.reshape(1, row_count),
        timesteps.reshape(1, samples),
        w_mod,
    )


def shards(query_rows, key_rows, value_rows, seg_ids, timesteps, w_mod):
    count = lax.axis_size("dp") * lax.axis_size("seq")
    whole_heads = query_rows.shape[1] == count * HEAD_DIM
    slab = count // QUARTERS
    even_slabs = count == slab * QUARTERS and slab & (slab - 1) == 0 and slab > 1
    body = head_shards if whole_heads and even_slabs else routed_shards
    return body(query_rows, key_rows, value_rows, seg_ids, timesteps, w_mod)


def solution(mesh):
    placed = (
        P(("dp", "seq"), None),
        P(("dp", "seq"), None),
        P(("dp", "seq"), None),
        P(("dp", "seq")),
        P(),
        P(),
    )
    return jax.shard_map(
        shards, mesh=mesh, in_specs=placed, out_specs=P(("dp", "seq"), None), check_vma=False
    )
```

```python
import functools
import math

import jax
import jax.numpy as jnp
from jax import lax
from jax.experimental import pallas as pl
from jax.experimental.pallas import tpu as pltpu
from jax.sharding import PartitionSpec as P

HEAD_DIM = 128
FREQ = 256
SEG_BIN = 2


def for_sending(value):
    return jax.tree.map(lambda a: a.astype(jnp.bfloat16) if a.dtype == jnp.float32 else a, value)


def scale_rows_table(timesteps, w_mod):
    half_freq = FREQ // 2
    frequencies = jnp.exp(-math.log(10000.0) * jnp.arange(half_freq, dtype=jnp.float32) / half_freq)
    angles = timesteps.astype(jnp.float32)[:, None] * frequencies[None, :]
    embedding = jnp.concatenate([jnp.cos(angles), jnp.sin(angles)], axis=1)
    activated = jax.nn.silu(embedding).astype(jnp.bfloat16)
    return jnp.dot(activated, w_mod, preferred_element_type=jnp.float32)


def slot_places(row_bins, bin_count, capacity):
    bin_hits = (row_bins[:, None] == jnp.arange(bin_count, dtype=jnp.int32)[None, :]).astype(
        jnp.int32
    )
    ranks = jnp.cumsum(bin_hits, axis=0) - bin_hits
    slot_rank = jnp.sum(ranks * bin_hits, axis=1)
    target = row_bins * capacity + slot_rank
    return jnp.arange(bin_count * capacity, dtype=jnp.int32)[:, None] == target[None, :]


def slot_ids_of(placement, sample_ids):
    return jnp.sum(jnp.where(placement, sample_ids[None, :] + 1, 0), axis=1) - 1


def attend_slots(query_part, key_part, value_part, sample_ids):
    length, row_width = query_part.shape
    head_count = row_width // HEAD_DIM
    block_rows = min(512, length)
    score_scale = 1.0 / math.sqrt(HEAD_DIM)
    query_blocks = query_part.reshape(length // block_rows, block_rows, head_count, HEAD_DIM)
    key_heads = key_part.reshape(length, head_count, HEAD_DIM)
    value_heads = value_part.reshape(length, head_count, HEAD_DIM)
    id_blocks = sample_ids.reshape(length // block_rows, block_rows)

    def one_block(block_pair):
        query_block, query_ids = block_pair
        scores = (
            jnp.einsum("qhd,khd->hqk", query_block, key_heads, preferred_element_type=jnp.float32)
            * score_scale
        )
        same_sample = query_ids[:, None] == sample_ids[None, :]
        scores = jnp.where(same_sample[None], scores, -1e30)
        row_max = jnp.max(scores, axis=2, keepdims=True)
        weights = jnp.exp(scores - row_max)
        soft_probs = (weights / jnp.sum(weights, axis=2, keepdims=True)).astype(jnp.bfloat16)
        block_out = jnp.einsum(
            "hqk,khd->qhd", soft_probs, value_heads, preferred_element_type=jnp.float32
        )
        return block_out.astype(jnp.bfloat16).reshape(block_rows, row_width)

    return lax.map(one_block, (query_blocks, id_blocks)).reshape(length, row_width)


def place_rows(place_mask, arrays):
    return tuple(
        (
            jnp.dot(place_mask, single, preferred_element_type=jnp.float32).astype(jnp.bfloat16)
            for single in arrays
        )
    )


def routed_shards(query_rows, key_rows, value_rows, seg_ids, timesteps, w_mod):
    dp_count = lax.axis_size("dp")
    seq_count = lax.axis_size("seq")
    row_count = query_rows.shape[0]
    capacity = 2 * row_count // dp_count
    ids_tiled = jnp.broadcast_to(seg_ids[:, None], (row_count, seq_count))
    group_ids = lax.all_to_all(ids_tiled, "seq", split_axis=1, concat_axis=0, tiled=True).reshape(
        -1
    )
    head_parts = (
        lax.all_to_all(query_rows, "seq", split_axis=1, concat_axis=0, tiled=True),
        lax.all_to_all(key_rows, "seq", split_axis=1, concat_axis=0, tiled=True),
        lax.all_to_all(value_rows, "seq", split_axis=1, concat_axis=0, tiled=True),
    )
    placement = slot_places(group_ids // SEG_BIN, dp_count, seq_count * capacity)
    place_mask = placement.astype(jnp.bfloat16)
    slotted = place_rows(place_mask, head_parts)
    bin_ids = lax.all_to_all(
        slot_ids_of(placement, group_ids), "dp", split_axis=0, concat_axis=0, tiled=True
    )
    bin_query, bin_key, bin_value = jax.tree.map(
        lambda part, own: part.astype(own.dtype),
        lax.all_to_all(for_sending(slotted), "dp", split_axis=0, concat_axis=0, tiled=True),
        slotted,
    )
    attended = attend_slots(bin_query, bin_key, bin_value, bin_ids)
    returned = lax.all_to_all(attended, "dp", split_axis=0, concat_axis=0, tiled=True)
    unslotted = jnp.dot(place_mask.T, returned, preferred_element_type=jnp.float32).astype(
        jnp.bfloat16
    )
    home_rows = lax.all_to_all(unslotted, "seq", split_axis=0, concat_axis=1, tiled=True)
    scale_table = scale_rows_table(timesteps, w_mod)
    lookup = (
        seg_ids[:, None] == jnp.arange(scale_table.shape[0], dtype=jnp.int32)[None, :]
    ).astype(jnp.float32)
    row_scales = jnp.dot(
        lookup, scale_table, precision=lax.Precision.HIGHEST, preferred_element_type=jnp.float32
    )
    return (home_rows.astype(jnp.float32) * (1.0 + row_scales)).astype(jnp.bfloat16)


EXCLUDED = float(1 << 20)
NT = (((1,), (1,)), ((), ()))
TN = (((0,), (0,)), ((), ()))
QUARTERS = 4


def head_kernel(
    sizes,
    q_ref,
    k_ref,
    v_ref,
    ids_ref,
    times_ref,
    w_ref,
    out_ref,
    rows_buf,
    ids_buf,
    times_buf,
    w_buf,
    table_buf,
    place_buf,
    q_slots,
    k_slots,
    v_slots,
    group_out,
    out_buf,
    sem_send,
    sem_recv,
    sem_side,
    sweep,
    line,
):
    dp_count, seq_count, capacity = sizes
    count = dp_count * seq_count
    slab = count // QUARTERS
    row_count = out_ref.shape[0]
    slot_count = dp_count * capacity
    me = lax.axis_index("dp") * seq_count + lax.axis_index("seq")
    quarter = me // slab
    spot = me % slab
    inner = (quarter == 1) | (quarter == 2)
    outer = (quarter == 0) | (quarter == 3)
    partner = quarter + 1 - 2 * (quarter % 2)
    across = QUARTERS - 1 - quarter
    beyond = QUARTERS - 1 - partner
    sources = (k_ref, v_ref, q_ref)

    def device_of(index):
        return (index // seq_count, index % seq_count)

    def mixed_spot(step):
        total, bit = 0, 1
        while bit < slab:
            total = total + (spot // bit + step // bit) % 2 * bit
            bit *= 2
        return total

    def at_spot(of_quarter, step):
        return of_quarter * slab + mixed_spot(step)

    def head_columns(index):
        return pl.ds(pl.multiple_of(index * HEAD_DIM, HEAD_DIM), HEAD_DIM)

    def part_copy(part, target):
        return pltpu.make_async_remote_copy(
            src_ref=sources[part].at[:, head_columns(target)],
            dst_ref=rows_buf.at[part, me],
            send_sem=sem_send.at[part],
            recv_sem=sem_recv.at[part, quarter],
            device_id=device_of(target),
            device_id_type=pl.DeviceIdType.MESH,
        )

    def ids_copy(target):
        return pltpu.make_async_remote_copy(
            src_ref=ids_ref,
            dst_ref=ids_buf.at[me],
            send_sem=sem_send.at[3],
            recv_sem=sem_recv.at[3, quarter],
            device_id=device_of(target),
            device_id_type=pl.DeviceIdType.MESH,
        )

    def out_copy(target):
        return pltpu.make_async_remote_copy(
            src_ref=out_buf.at[target],
            dst_ref=out_ref.at[:, head_columns(me)],
            send_sem=sem_send.at[4],
            recv_sem=sem_side.at[0],
            device_id=device_of(target),
            device_id_type=pl.DeviceIdType.MESH,
        )

    def own_out():
        return pltpu.make_async_copy(
            out_buf.at[me], out_ref.at[:, head_columns(me)], sem_side.at[0]
        )

    def wait_for(region, sem):
        pltpu.make_async_copy(region, region, sem).wait()

    def slab_of(of_quarter):
        return pl.ds(pl.multiple_of(of_quarter * slab, slab), slab)

    def tell(sem, target):
        pl.semaphore_signal(
            sem, inc=1, device_id=device_of(target), device_id_type=pl.DeviceIdType.MESH
        )

    def send(part, target):
        if part == 0:
            ids_copy(target).start()
        part_copy(part, target).start()

    barrier = pltpu.get_barrier_semaphore()
    pair = min(2, slab)
    bits = [1 << n for n in range(slab.bit_length() - 1)]

    @pl.when(inner)
    def _():
        for step in range(pair):
            tell(barrier, at_spot(across, step))
        for step in range(pair):
            tell(barrier, at_spot(partner, step))

    for bit in bits:
        tell(barrier, at_spot(quarter, bit))

    for part in range(3):
        pltpu.make_async_copy(
            sources[part].at[:, head_columns(me)], rows_buf.at[part, me], sem_recv.at[part, quarter]
        ).start()
    pltpu.make_async_copy(ids_ref, ids_buf.at[me], sem_recv.at[3, quarter]).start()
    times_copy = pltpu.make_async_copy(times_ref, times_buf, sem_side.at[1])
    w_copy = pltpu.make_async_copy(w_ref.at[:, head_columns(me)], w_buf, sem_side.at[2])
    times_copy.start()
    w_copy.start()

    pl.semaphore_wait(barrier, len(bits) + pair)

    @pl.when(inner)
    def _():
        for part in range(2):
            for step in range(pair):
                send(part, at_spot(across, step))

    for n, bit in enumerate(bits[1:]):
        tell(sweep.at[n], at_spot(quarter, bit))
        pl.semaphore_wait(sweep.at[n], 1)

    def send_rounds(*streams):
        @pl.loop(0, slab)
        def _(step):
            for part, of_quarter in streams:
                if of_quarter is quarter:
                    first = 1
                elif of_quarter is across and part < 2:
                    first = jnp.where(inner, pair, 0)
                else:
                    first = 0

                @pl.when((step >= first) if part < 2 else (slab - 1 - step >= first))
                def _():
                    send(part, at_spot(of_quarter, jnp.where(part == 2, slab - 1 - step, step)))

    @pl.when(outer)
    def _():
        tell(line.at[0], at_spot(partner, 0))
        pl.semaphore_wait(line.at[0], 1)
        send_rounds((0, across), (0, partner))
        send_rounds((0, beyond), (0, quarter))
        send_rounds((1, across), (1, partner))
        send_rounds((1, beyond), (1, quarter))
        send_rounds((2, across), (2, partner))
        send_rounds((2, beyond), (2, quarter))

    @pl.when(inner)
    def _():
        send_rounds((0, across))
        pl.semaphore_wait(line.at[0], 1)
        tell(line.at[1], at_spot(across, 0))
        send_rounds((0, partner), (1, across))
        send_rounds((1, partner))
        pl.semaphore_wait(line.at[1], 1)
        tell(line.at[0], at_spot(partner, 0))
        send_rounds((0, beyond), (0, quarter))
        send_rounds((1, beyond), (1, quarter))
        send_rounds((2, partner), (2, quarter))

    times_copy.wait()
    samples = times_buf.shape[1]
    square = (samples, samples)
    diagonal = lax.broadcasted_iota(jnp.int32, square, 0) == lax.broadcasted_iota(
        jnp.int32, square, 1
    )
    times = jnp.broadcast_to(times_buf[...].astype(jnp.float32), square)
    times = jnp.sum(jnp.where(diagonal, times, 0.0), axis=1, keepdims=True)
    half_freq = FREQ // 2
    ramp = lax.broadcasted_iota(jnp.int32, (1, half_freq), 1).astype(jnp.float32)
    angles = times * jnp.exp(-math.log(10000.0) * ramp / half_freq)
    waves = (jax.nn.silu(wave(angles)).astype(jnp.bfloat16) for wave in (jnp.cos, jnp.sin))
    w_copy.wait()
    table_buf[...] = sum(
        jnp.dot(
            wave, w_buf[n * half_freq : (n + 1) * half_freq, :], preferred_element_type=jnp.float32
        )
        for n, wave in enumerate(waves)
    )

    v_slots[:, :, HEAD_DIM:] = jnp.ones((dp_count, count * capacity, HEAD_DIM), jnp.bfloat16)
    before = (
        lax.broadcasted_iota(jnp.int32, (row_count, row_count), 0)
        < lax.broadcasted_iota(jnp.int32, (row_count, row_count), 1)
    ).astype(jnp.bfloat16)
    part_lane = lax.broadcasted_iota(jnp.int32, (1, HEAD_DIM), 1) < SEG_BIN

    def member_hits(origin):
        ids = ids_buf[origin]
        member = ids - ids // SEG_BIN * SEG_BIN
        return lax.broadcasted_iota(jnp.int32, (HEAD_DIM, row_count), 0) == member

    def marks_of(place, hits):
        return lax.dot_general(
            place, hits.astype(jnp.bfloat16), NT, preferred_element_type=jnp.float32
        )

    def placed_part(place, origin, part):
        return jnp.dot(place, rows_buf[part, origin], preferred_element_type=jnp.float32)

    def by_bin(value):
        return value.astype(jnp.bfloat16).reshape((dp_count, capacity, HEAD_DIM))

    def slots_at(index):
        return pl.ds(pl.multiple_of(index * capacity, capacity), capacity)

    def place_k(origin):
        bins = ids_buf[origin] // SEG_BIN
        bin_hits = lax.broadcasted_iota(jnp.int32, (16, row_count), 0) == bins
        ranks = jnp.dot(
            bin_hits.astype(jnp.bfloat16), before, preferred_element_type=jnp.float32
        )
        rank = jnp.sum(jnp.where(bin_hits, ranks, 0.0), axis=0, keepdims=True)
        slot = bins * capacity + rank.astype(jnp.int32)
        place = (
            lax.broadcasted_iota(jnp.int32, (slot_count, row_count), 0) == slot
        ).astype(jnp.bfloat16)
        place_buf[origin] = place
        other_member = marks_of(place, jnp.logical_not(member_hits(origin)))
        k_marks = jnp.where(part_lane, 1.0 - other_member, 0.0)
        k_slots[:, slots_at(origin), :HEAD_DIM] = by_bin(placed_part(place, origin, 0))
        k_slots[:, slots_at(origin), HEAD_DIM:] = by_bin(k_marks)

    def place_v(origin):
        placed = placed_part(place_buf[origin], origin, 1)
        v_slots[:, slots_at(origin), :HEAD_DIM] = by_bin(placed)

    def place_q(origin, inner_index):
        place = place_buf[origin]
        own_member = marks_of(place, member_hits(origin))
        q_marks = jnp.where(part_lane, (own_member - 1.0) * EXCLUDED, 0.0)
        at = slice(inner_index * capacity, (inner_index + 1) * capacity)
        q_slots[:, at, :HEAD_DIM] = by_bin(placed_part(place, origin, 2))
        q_slots[:, at, HEAD_DIM:] = by_bin(q_marks)

    def arrived(part, of_quarter):
        wait_for(rows_buf.at[part, slab_of(of_quarter)], sem_recv.at[part, of_quarter])

    def turn_quarter(turn, order):
        found = order[-1]
        for n in range(len(order) - 1):
            found = jnp.where(turn == n, order[n], found)
        return found

    arrivals = (
        partner,
        jnp.where(inner, across, quarter),
        jnp.where(inner, quarter, beyond),
        jnp.where(inner, beyond, across),
    )
    queries = (
        partner,
        jnp.where(inner, beyond, across),
        quarter,
        jnp.where(inner, across, beyond),
    )

    @pl.loop(0, 2)
    def _(stage):
        @pl.loop(2 * stage, 2 * stage + 2)
        def _(turn):
            of_quarter = turn_quarter(turn, arrivals)
            wait_for(ids_buf.at[slab_of(of_quarter)], sem_recv.at[3, of_quarter])
            arrived(0, of_quarter)

            @pl.loop(0, slab)
            def _(n):
                place_k(of_quarter * slab + n)

        @pl.loop(2 * stage, 2 * stage + 2)
        def _(turn):
            of_quarter = turn_quarter(turn, arrivals)
            arrived(1, of_quarter)

            @pl.loop(0, slab)
            def _(n):
                place_v(of_quarter * slab + n)

    @pl.when(inner)
    def _():
        send_rounds((2, beyond))

    exponent_scale = 1.0 / (math.sqrt(HEAD_DIM) * math.log(2.0))
    group_slots = slab * capacity

    @pl.loop(0, QUARTERS)
    def _(turn):
        of_quarter = turn_quarter(turn, queries)
        arrived(2, of_quarter)

        @pl.when(inner & (turn == 1))
        def _():
            send_rounds((2, across))

        for n in range(slab):
            place_q(at_spot(of_quarter, slab - 1 - n), n)

        @pl.loop(0, dp_count, unroll=8)
        def _(bin_index):
            query = q_slots[bin_index]
            scores = lax.dot_general(
                query, k_slots[bin_index], NT, preferred_element_type=jnp.float32
            )
            row_max = jnp.max(scores, axis=1, keepdims=True)
            weights = jnp.exp2((scores - row_max) * exponent_scale).astype(jnp.bfloat16)
            sums = jnp.dot(weights, v_slots[bin_index], preferred_element_type=jnp.float32)
            attended = (sums[:, :HEAD_DIM] / sums[:, HEAD_DIM:]).astype(jnp.bfloat16)
            factor = jnp.zeros((group_slots, HEAD_DIM), jnp.float32)
            for member in range(SEG_BIN):
                mark = query[:, HEAD_DIM + member : HEAD_DIM + member + 1].astype(jnp.float32)
                row = table_buf[pl.ds(bin_index * SEG_BIN + member, 1), :]
                factor = jnp.where(mark == 0.0, 1.0 + row, factor)
            mixed = (attended.astype(jnp.float32) * factor).astype(jnp.bfloat16)
            group_out[bin_index] = mixed

        for n in range(slab):
            target = at_spot(of_quarter, slab - 1 - n)
            slots = group_out[:, n * capacity : (n + 1) * capacity, :].reshape(
                (slot_count, HEAD_DIM)
            )
            out_buf[target] = lax.dot_general(
                place_buf[target], slots, TN, preferred_element_type=jnp.float32
            ).astype(jnp.bfloat16)

            @pl.when(target == me)
            def _():
                own_out().start()

            @pl.when(target != me)
            def _():
                out_copy(target).start()

    others = pl.ds(0, (count - 1) * HEAD_DIM)
    for part in range(3):
        wait_for(sources[part].at[:, others], sem_send.at[part])
    wait_for(ids_buf.at[pl.ds(0, count - 1)], sem_send.at[3])
    wait_for(out_buf.at[pl.ds(0, count - 1)], sem_send.at[4])
    wait_for(out_ref, sem_side.at[0])


def head_shards(query_rows, key_rows, value_rows, seg_ids, timesteps, w_mod):
    dp_count = lax.axis_size("dp")
    seq_count = lax.axis_size("seq")
    count = dp_count * seq_count
    row_count, width = query_rows.shape
    samples = timesteps.shape[0]
    capacity = 2 * row_count // dp_count
    slab = count // QUARTERS
    anywhere = pl.BlockSpec(memory_space=pl.ANY)
    slots = (dp_count, count * capacity, 2 * HEAD_DIM)
    return pl.pallas_call(
        functools.partial(head_kernel, (dp_count, seq_count, capacity)),
        out_shape=pltpu.VMEM((row_count, width), jnp.bfloat16),
        in_specs=[anywhere] * 6,
        out_specs=pl.BlockSpec(memory_space=pltpu.VMEM),
        scratch_shapes=[
            pltpu.VMEM((3, count, row_count, HEAD_DIM), jnp.bfloat16),
            pltpu.VMEM((count, 1, row_count), jnp.int32),
            pltpu.VMEM((1, samples), jnp.int32),
            pltpu.VMEM((FREQ, HEAD_DIM), jnp.bfloat16),
            pltpu.VMEM((samples, HEAD_DIM), jnp.float32),
            pltpu.VMEM((count, dp_count * capacity, row_count), jnp.bfloat16),
            pltpu.VMEM((dp_count, slab * capacity, 2 * HEAD_DIM), jnp.bfloat16),
            pltpu.VMEM(slots, jnp.bfloat16),
            pltpu.VMEM(slots, jnp.bfloat16),
            pltpu.VMEM((dp_count, slab * capacity, HEAD_DIM), jnp.bfloat16),
            pltpu.VMEM((count, row_count, HEAD_DIM), jnp.bfloat16),
            pltpu.SemaphoreType.DMA((5,)),
            pltpu.SemaphoreType.DMA((4, QUARTERS)),
            pltpu.SemaphoreType.DMA((3,)),
            pltpu.SemaphoreType.REGULAR((slab.bit_length(),)),
            pltpu.SemaphoreType.REGULAR((2,)),
        ],
        compiler_params=pltpu.CompilerParams(
            collective_id=0, has_side_effects=True, vmem_limit_bytes=56 * 1024 * 1024
        ),
    )(
        query_rows,
        key_rows,
        value_rows,
        seg_ids.reshape(1, row_count),
        timesteps.reshape(1, samples),
        w_mod,
    )


def shards(query_rows, key_rows, value_rows, seg_ids, timesteps, w_mod):
    count = lax.axis_size("dp") * lax.axis_size("seq")
    whole_heads = query_rows.shape[1] == count * HEAD_DIM
    slab = count // QUARTERS
    even_slabs = count == slab * QUARTERS and slab & (slab - 1) == 0 and slab > 1
    body = head_shards if whole_heads and even_slabs else routed_shards
    return body(query_rows, key_rows, value_rows, seg_ids, timesteps, w_mod)


def solution(mesh):
    placed = (
        P(("dp", "seq"), None),
        P(("dp", "seq"), None),
        P(("dp", "seq"), None),
        P(("dp", "seq")),
        P(),
        P(),
    )
    return jax.shard_map(
        shards, mesh=mesh, in_specs=placed, out_specs=P(("dp", "seq"), None), check_vma=False
    )
```
